256 devices in a mesh: dp: 16 (over x, y), tensor: 16 (over z, core).
Axes of the slice: x: 4, y: 4, z: 8, core: 2. Of those that a mesh axis runs over, the one named last changes fastest.
Arguments:
- attention_output: bfloat16 [2048, 8192], P('dp', 'tensor'), may hold values from -6 to 6
- residual: bfloat16 [2048, 8192], P('dp', 'tensor'), may hold values from -6 to 6
- output_weight: bfloat16 [8192, 8192], P('tensor'), may hold values from -0.09375 to 0.09375
- down_factors: bfloat16 [1024, 8192, 16], P('dp', 'tensor'), may hold values from -0.0625 to 0.0625
- up_factors: bfloat16 [1024, 16, 8192], P('dp', None, 'tensor'), may hold values from -1.5 to 1.5
- adapter_index: int32 [2048], P('dp'), may hold values from 0 to 1023, as said below
Outputs:
- layer_out: bfloat16 [2048, 8192], P('dp', 'tensor')
The draws below stay inside these ranges and needn't reach their ends.
Inputs may be any that keep to these rules, and one draw needn't show every extreme that they name: adapter_index // 64 is the request group that owns the adapter. Of one group's 128 rows at most 16 use adapters owned by one group, and in every draw some group owns the adapters of exactly 16 rows of every group.
All inputs are finite; a program needn't handle non-finite values.
Results may differ from the reference program's by a relative error of at most 0.0041.
Values may be sent and summed in bfloat16 or wider, within the bound.
No kernel may reach another device: no remote copies, remote signals or barrier semaphores. Data moves between devices by JAX's collectives and lax.ppermute only.
A program may use at most 64 MiB of HBM per device.

```python
import jax
import jax.numpy as jnp
from jax import lax

MODEL_WIDTH = 8192
ADAPTER_RANK = 16
ADP_DEV = 64
ROWS = 128
ATTENTION_WIDTH = 8192
ADAPTER_COUNT = 1024
CAP = 16
ROWS_ALL = 2048
N_DP = 16


def draw_adapter_index(key, part):
    hot_key = jax.random.fold_in(key, 11)
    group_key = jax.random.fold_in(key, 23)
    hot_group = jax.random.randint(hot_key, (), 0, N_DP)

    def one_group(group_index):
        base_key = jax.random.fold_in(group_key, group_index)
        key_one = jax.random.fold_in(base_key, 1)
        key_two = jax.random.fold_in(base_key, 2)
        key_three = jax.random.fold_in(base_key, 3)
        key_four = jax.random.fold_in(base_key, 4)
        others = (hot_group + 1 + jnp.arange((N_DP - 1) * CAP) // CAP) % N_DP
        others = jax.random.permutation(key_one, others)[:ROWS - CAP]
        owners = jnp.concatenate([jnp.full((CAP,), hot_group, jnp.int32), others.astype(jnp.int32)])
        owners = jax.random.permutation(key_two, owners)
        top_bound = jax.random.randint(key_three, (ROWS,), 1, ADP_DEV + 1)
        local_index = jax.random.randint(key_four, (ROWS,), 0, ADP_DEV) % top_bound
        return owners * ADP_DEV + local_index
    table = jax.vmap(one_group)(jnp.arange(N_DP))
    return table.reshape(-1).astype(jnp.int32)


def strengthened(result, rng, source, target, parts, factor):
    def block_of(dim):
        return (jnp.arange(result.shape[dim]) // (result.shape[dim] // parts)).reshape((-1,) + (1,) * (result.ndim - 1 - dim))

    near = jax.random.permutation(rng, parts)[block_of(target)]
    far = (block_of(target) + parts // 2) % parts
    return jnp.where((block_of(source) == near) | (block_of(source) == far), factor * result, result)


def levels(stream_key, dims, cuts, least, high):
    loudness, own = 1.0, jax.random.fold_in(stream_key, 6)
    for axis_at, parts in cuts:
        steps = jnp.exp(jax.random.uniform(jax.random.fold_in(own, axis_at), (parts,), jnp.float32, least / len(cuts), high / len(cuts)))
        loudness = loudness * jnp.repeat(steps, dims[axis_at] // parts).reshape([-1 if axis == axis_at else 1 for axis in range(len(dims))])
    return loudness


def bell_draw(key, shape, scale, limit, cuts=(), kind=jnp.bfloat16):
    level = levels(key, shape, cuts, -0.22, 0.18) if cuts else 1.0
    result = jax.random.normal(key, shape, jnp.float32) * scale * level
    return jnp.minimum(jnp.maximum(result, -limit), limit).astype(kind)


def noise_with(stream_key, dims, deviation, reach, pieces, heavy, dtype=jnp.bfloat16):
    values = deviation * jax.random.normal(stream_key, dims, jnp.float32)
    if pieces:
        values = values * levels(stream_key, dims, pieces, -0.22, 0.18)
    return jnp.clip(strengthened(values, jax.random.fold_in(stream_key, 3), *heavy), -reach, reach).astype(dtype)


def setup_inputs(seed: int = 0) -> dict:
    keys = jax.random.split(jax.random.key(seed), 7)
    attention_output = bell_draw(keys[0], (ROWS_ALL, ATTENTION_WIDTH), 1.0, 6.0, ((0, 16), (1, 16)))
    residual = bell_draw(keys[1], (ROWS_ALL, MODEL_WIDTH), 1.0, 6.0, ((0, 16), (1, 16)))
    output_weight = noise_with(keys[2], (ATTENTION_WIDTH, MODEL_WIDTH), ATTENTION_WIDTH ** -0.5, 0.09375, ((0, 16),), (0, 1, 16, 2.0))
    down_factors = bell_draw(keys[3], (ADAPTER_COUNT, ATTENTION_WIDTH, ADAPTER_RANK), ATTENTION_WIDTH ** -0.5, 0.0625, ((0, 16), (1, 16)))
    up_factors = bell_draw(keys[4], (ADAPTER_COUNT, ADAPTER_RANK, MODEL_WIDTH), ADAPTER_RANK ** -0.5, 1.5, ((0, 16), (2, 16)))
    adapter_index = draw_adapter_index(jax.random.fold_in(keys[6], 71), 0)
    return {"attention_output": attention_output, "residual": residual, "output_weight": output_weight, "down_factors": down_factors, "up_factors": up_factors, "adapter_index": adapter_index}


def reference(attention_output, residual, output_weight, down_factors, up_factors, adapter_index):
    base_out = jnp.dot(attention_output, output_weight, preferred_element_type=jnp.float32)
    blocks = ROWS_ALL // ROWS

    def branch(block_in):
        x_rows, row_indices = block_in
        selected_down = down_factors[row_indices].astype(jnp.float32)
        shrink = jnp.einsum("rk,rkj->rj", x_rows.astype(jnp.float32), selected_down).astype(jnp.bfloat16)
        selected_up = up_factors[row_indices].astype(jnp.float32)
        return jnp.einsum("rj,rjc->rc", shrink.astype(jnp.float32), selected_up).astype(jnp.bfloat16)

    expand = lax.map(branch, (attention_output.reshape(blocks, ROWS, ATTENTION_WIDTH), adapter_index.reshape(blocks, ROWS)))
    expand = expand.reshape(ROWS_ALL, MODEL_WIDTH)
    total = residual.astype(jnp.float32) + base_out + expand.astype(jnp.float32)
    return total.astype(jnp.bfloat16)
```

```python
import functools

import jax
import jax.numpy as jnp
from jax import lax
from jax.experimental import pallas as pl
from jax.experimental.pallas import tpu as pltpu
from jax.sharding import PartitionSpec as P

BF16 = jnp.bfloat16
F32 = jnp.float32
LANES = 128
RIGHT = (1, 4, -2)
LEFT = (-1, 2)
KEEP = (0, 3, -3)
GRANT = pltpu.CompilerParams(vmem_limit_bytes=16 * 2**20)


def vmem_specs(count):
    return [pl.BlockSpec(memory_space=pltpu.VMEM)] * count


def slots_of(index_row, owned, capacity):
    rows = index_row.shape[1]
    owner = index_row // owned
    owner_across = jnp.broadcast_to(owner, (rows, rows))
    owner_down = owner_across.T
    earlier = lax.broadcasted_iota(jnp.int32, (rows, rows), 0) < lax.broadcasted_iota(
        jnp.int32, (rows, rows), 1
    )
    same = jnp.where((owner_down == owner_across) & earlier, 1, 0)
    rank = jnp.sum(same, axis=0, keepdims=True)
    return owner * capacity + rank


def dispatch_kernel(owned, capacity, index_ref, x_ref, out_ref):
    index_row = index_ref[...]
    rows, width = x_ref.shape
    slot_count = out_ref.shape[0]
    slot = slots_of(index_row, owned, capacity)
    placing = lax.broadcasted_iota(jnp.int32, (slot_count, rows), 0) == slot
    out_ref[:, :width] = jnp.dot(
        jnp.where(placing, 1.0, 0.0).astype(BF16), x_ref[...], preferred_element_type=F32
    ).astype(BF16)
    number = (index_row % owned + 1).astype(F32)
    asked = jnp.sum(jnp.where(placing, number, 0.0), axis=1, keepdims=True)
    out_ref[:, width:] = jnp.broadcast_to(asked, (slot_count, LANES)).astype(BF16)


def dispatch(index_row, x, owned, capacity, slot_count):
    rows, width = x.shape
    return pl.pallas_call(
        functools.partial(dispatch_kernel, owned, capacity),
        out_shape=jax.ShapeDtypeStruct((slot_count, width + LANES), BF16),
        in_specs=vmem_specs(2),
        out_specs=pl.BlockSpec(memory_space=pltpu.VMEM),
        cost_estimate=pl.CostEstimate(
            flops=2 * slot_count * rows * width, bytes_accessed=2 * slot_count * width, transcendentals=0
        ),
        compiler_params=GRANT,
        name="dispatch",
    )(index_row, x)


def product_kernel(half_ref, x_ref, w_ref, out_ref):
    out_ref[0] = jnp.dot(x_ref[...], w_ref[...], preferred_element_type=F32).astype(out_ref.dtype)


def half_product(x, w, parity, chips, out_dtype, name):
    rows, depth = x.shape
    block = w.shape[1] // (2 * chips)
    return pl.pallas_call(
        product_kernel,
        out_shape=jax.ShapeDtypeStruct((chips, rows, block), out_dtype),
        grid_spec=pltpu.PrefetchScalarGridSpec(
            num_scalar_prefetch=1,
            grid=(chips,),
            in_specs=[
                pl.BlockSpec((rows, depth), lambda i, half: (0, 0)),
                pl.BlockSpec((depth, block), lambda i, half: (0, 2 * i + half[0])),
            ],
            out_specs=pl.BlockSpec((1, rows, block), lambda i, half: (i, 0, 0)),
        ),
        cost_estimate=pl.CostEstimate(
            flops=2 * rows * depth * block * chips,
            bytes_accessed=2 * depth * block * chips,
            transcendentals=0,
        ),
        compiler_params=pltpu.CompilerParams(vmem_limit_bytes=56 * 2**20),
        name=name,
    )(parity, x, w)


def pair_kernel(chips, z_ref, mine_ref, other_ref, right_ref, left_ref, keep_ref):
    z = z_ref[0]
    for refs, steps in ((right_ref, RIGHT), (left_ref, LEFT), (keep_ref, KEEP)):
        for place, step in enumerate(steps):
            at = lax.rem(z + (step + chips), chips)
            total = mine_ref[at] + other_ref[at].astype(F32)
            refs[place] = total.astype(refs.dtype)


def pair_sum(z, mine, other):
    chips, rows, block = mine.shape
    return pl.pallas_call(
        functools.partial(pair_kernel, chips),
        out_shape=(
            jax.ShapeDtypeStruct((len(RIGHT), rows, block), BF16),
            jax.ShapeDtypeStruct((len(LEFT), rows, block), BF16),
            jax.ShapeDtypeStruct((len(KEEP), rows, block), F32),
        ),
        in_specs=[pl.BlockSpec(memory_space=pltpu.SMEM)] + vmem_specs(2),
        out_specs=tuple(vmem_specs(3)),
        cost_estimate=pl.CostEstimate(flops=mine.size, bytes_accessed=8 * mine.size, transcendentals=0),
        compiler_params=GRANT,
        name="pair_sum",
    )(z, mine, other)


def relay_kernel(keep_ref, right_ref, left_ref, here_ref, far_right_ref, far_left_ref):
    here_ref[...] = keep_ref[0] + right_ref[0].astype(F32) + left_ref[0].astype(F32)
    far_right_ref[...] = (
        keep_ref[1] + right_ref[1].astype(F32) + left_ref[1].astype(F32)
    ).astype(BF16)
    far_left_ref[...] = (keep_ref[2] + right_ref[2].astype(F32)).astype(BF16)


def relay(keep, right, left):
    _, rows, block = keep.shape
    return pl.pallas_call(
        relay_kernel,
        out_shape=(
            jax.ShapeDtypeStruct((rows, block), F32),
            jax.ShapeDtypeStruct((rows, block), BF16),
            jax.ShapeDtypeStruct((rows, block), BF16),
        ),
        in_specs=vmem_specs(3),
        out_specs=tuple(vmem_specs(3)),
        cost_estimate=pl.CostEstimate(flops=5 * rows * block, bytes_accessed=4 * keep.size, transcendentals=0),
        compiler_params=GRANT,
        name="relay",
    )(keep, right, left)


def wanted_row(slots_ref, width):
    tags = slots_ref[:, width:].astype(F32)
    return tags.T[0:1, :]


def shrink_kernel(owned, copies, slots_ref, down_ref, out_ref):
    slot_total = slots_ref.shape[0]
    width = down_ref.shape[1]
    rank = down_ref.shape[0] // owned
    terms = lax.dot_general(
        down_ref[...], slots_ref[:, :width], (((1,), (1,)), ((), ())), preferred_element_type=F32
    )
    wanted = wanted_row(slots_ref, width)
    total = jnp.zeros((rank, slot_total), F32)
    for adapter in range(owned):
        total += jnp.where(wanted == adapter + 1, terms[adapter * rank : (adapter + 1) * rank], 0.0)
    for copy in range(copies):
        out_ref[copy] = total


def shrink_terms(slots, down, owned, copies):
    slot_total = slots.shape[0]
    rank = down.shape[0] // owned
    return pl.pallas_call(
        functools.partial(shrink_kernel, owned, copies),
        out_shape=jax.ShapeDtypeStruct((copies, rank, slot_total), F32),
        in_specs=vmem_specs(2),
        out_specs=pl.BlockSpec(memory_space=pltpu.VMEM),
        cost_estimate=pl.CostEstimate(
            flops=2 * slot_total * down.size, bytes_accessed=2 * down.size, transcendentals=0
        ),
        compiler_params=GRANT,
        name="shrink",
    )(slots, down)


def expand_kernel(owned, parts_ref, slots_ref, up_ref, out_ref):
    slot_total = slots_ref.shape[0]
    copies, rank, _ = parts_ref.shape
    total = parts_ref[0]
    for copy in range(1, copies):
        total += parts_ref[copy]
    shrink = total.astype(BF16).astype(F32)
    wanted = wanted_row(slots_ref, slots_ref.shape[1] - LANES)
    spread = jnp.concatenate(
        [jnp.where(wanted == adapter + 1, shrink, 0.0).astype(BF16) for adapter in range(owned)], axis=0
    )
    out_ref[...] = lax.dot_general(
        spread, up_ref[...], (((0,), (0,)), ((), ())), preferred_element_type=F32
    ).astype(BF16)


def expand_rows(parts, slots, up, owned):
    slot_total = slots.shape[0]
    return pl.pallas_call(
        functools.partial(expand_kernel, owned),
        out_shape=jax.ShapeDtypeStruct((slot_total, up.shape[1]), BF16),
        in_specs=vmem_specs(3),
        out_specs=pl.BlockSpec(memory_space=pltpu.VMEM),
        cost_estimate=pl.CostEstimate(
            flops=2 * slot_total * up.size, bytes_accessed=2 * up.size, transcendentals=0
        ),
        compiler_params=GRANT,
        name="expand",
    )(parts, slots, up)


def finish_kernel(
    owned, capacity, index_ref, residual_ref, here_ref, right_ref, left_ref, returned_ref, out_ref
):
    rows = residual_ref.shape[0]
    slot_count = returned_ref.shape[0]
    slot = slots_of(index_ref[...], owned, capacity)
    placing = lax.broadcasted_iota(jnp.int32, (slot_count, rows), 0) == slot
    branch = lax.dot_general(
        jnp.where(placing, 1.0, 0.0).astype(BF16),
        returned_ref[...],
        (((0,), (0,)), ((), ())),
        preferred_element_type=F32,
    )
    base = here_ref[...] + right_ref[...].astype(F32) + left_ref[...].astype(F32)
    out_ref[...] = (residual_ref[...].astype(F32) + base + branch).astype(BF16)


def finish(index_row, residual, sums, returned, owned, capacity):
    return pl.pallas_call(
        functools.partial(finish_kernel, owned, capacity),
        out_shape=jax.ShapeDtypeStruct(residual.shape, BF16),
        in_specs=vmem_specs(6),
        out_specs=pl.BlockSpec(memory_space=pltpu.VMEM),
        cost_estimate=pl.CostEstimate(
            flops=2 * returned.size * residual.shape[0], bytes_accessed=8 * residual.size, transcendentals=0
        ),
        compiler_params=GRANT,
        name="finish",
    )(index_row, residual, *sums, returned)


def body(attention_output, residual, output_weight, down_factors, up_factors, adapter_index):
    rows, width = attention_output.shape
    owned, _, rank = down_factors.shape
    columns = up_factors.shape[2]
    groups = lax.axis_size("dp")
    shards = lax.axis_size("tensor")
    chips = shards // 2
    capacity = 2 * rows // groups
    slot_count = groups * capacity
    place = lax.axis_index("tensor")
    z, core = (place >> 1).reshape(1), (place & 1).reshape(1)
    siblings = [(i, i ^ 1) for i in range(shards)]

    def along_z(array, step):
        return lax.ppermute(array, "tensor", [(i, (i + 2 * step) % shards) for i in range(shards)])

    index_row = adapter_index.reshape(1, rows)
    outgoing = dispatch(index_row, attention_output, owned, capacity, slot_count)
    outgoing, x = lax.optimization_barrier((outgoing, attention_output))
    outgoing = outgoing.reshape(groups, capacity, width + LANES)
    slots = lax.all_to_all(outgoing, "dp", split_axis=0, concat_axis=0, tiled=True)

    theirs = half_product(x, output_weight, 1 - core, chips, BF16, "product_theirs")
    other = lax.ppermute(theirs, "tensor", siblings)
    mine = half_product(x, output_weight, core, chips, F32, "product_mine")
    to_right, to_left, keep = pair_sum(z, mine, other)
    from_left, from_right = along_z(to_right, 1), along_z(to_left, -1)

    slots, keep = lax.optimization_barrier((slots, keep))
    slots = slots.reshape(slot_count, width + LANES)
    down = down_factors.transpose(0, 2, 1).reshape(owned * rank, width)
    parts = shrink_terms(slots, down, owned, shards)
    parts = lax.all_to_all(parts, "tensor", split_axis=0, concat_axis=0, tiled=True)
    here, far_right, far_left = relay(keep, from_left, from_right)
    sums = (here, along_z(far_right, 3), along_z(far_left, -3))
    expand = expand_rows(parts, slots, up_factors.reshape(owned * rank, columns), owned)
    expand = expand.reshape(groups, capacity, columns)
    returned = lax.all_to_all(expand, "dp", split_axis=0, concat_axis=0, tiled=True)
    returned = returned.reshape(slot_count, columns)
    return finish(index_row, residual, sums, returned, owned, capacity)


def solution(mesh):
    return jax.shard_map(
        body,
        mesh=mesh,
        in_specs=(
            P("dp", "tensor"),
            P("dp", "tensor"),
            P("tensor", None),
            P("dp", "tensor", None),
            P("dp", None, "tensor"),
            P("dp"),
        ),
        out_specs=P("dp", "tensor"),
        check_vma=False,
    )
```

```python
import functools

import jax
import jax.numpy as jnp
from jax import lax
from jax.experimental import pallas as pl
from jax.experimental.pallas import tpu as pltpu
from jax.sharding import PartitionSpec as P

BF16 = jnp.bfloat16
F32 = jnp.float32
LANES = 128
RIGHT = (1, -2)
LEFT = (-1, 2)
KEEP = (0, 3, -3)
PIECES = 8
GRANT = pltpu.CompilerParams(vmem_limit_bytes=16 * 2**20)
WHOLE = pltpu.CompilerParams(vmem_limit_bytes=60 * 2**20)


def vmem_specs(count):
    return [pl.BlockSpec(memory_space=pltpu.VMEM)] * count


def slots_of(index_row, owned, capacity):
    rows = index_row.shape[1]
    owner = index_row // owned
    owner_across = jnp.broadcast_to(owner, (rows, rows))
    owner_down = owner_across.T
    earlier = lax.broadcasted_iota(jnp.int32, (rows, rows), 0) < lax.broadcasted_iota(
        jnp.int32, (rows, rows), 1
    )
    same = jnp.where((owner_down == owner_across) & earlier, 1, 0)
    rank = jnp.sum(same, axis=0, keepdims=True)
    return owner * capacity + rank


def dispatch_kernel(owned, capacity, index_ref, x_ref, out_ref):
    index_row = index_ref[...]
    rows, width = x_ref.shape
    slot_count = out_ref.shape[0]
    slot = slots_of(index_row, owned, capacity)
    placing = lax.broadcasted_iota(jnp.int32, (slot_count, rows), 0) == slot
    out_ref[:, :width] = jnp.dot(
        jnp.where(placing, 1.0, 0.0).astype(BF16), x_ref[...], preferred_element_type=F32
    ).astype(BF16)
    number = (index_row % owned + 1).astype(F32)
    asked = jnp.sum(jnp.where(placing, number, 0.0), axis=1, keepdims=True)
    out_ref[:, width:] = jnp.broadcast_to(asked, (slot_count, LANES)).astype(BF16)


def dispatch(index_row, x, owned, capacity, slot_count):
    rows, width = x.shape
    return pl.pallas_call(
        functools.partial(dispatch_kernel, owned, capacity),
        out_shape=jax.ShapeDtypeStruct((slot_count, width + LANES), BF16),
        in_specs=vmem_specs(2),
        out_specs=pl.BlockSpec(memory_space=pltpu.VMEM),
        cost_estimate=pl.CostEstimate(
            flops=2 * slot_count * rows * width, bytes_accessed=2 * slot_count * width, transcendentals=0
        ),
        compiler_params=WHOLE,
        name="dispatch",
    )(index_row, x)


def product_kernel(
    core_ref, x_ref, w_hbm, theirs_hbm, mine_hbm, w_ref, theirs_ref, mine_ref, in_sems, theirs_sems, mine_sems
):
    first = core_ref[0] == 0
    chips, _, block = mine_ref.shape
    depth = w_ref.shape[0] // PIECES
    loads = []
    for piece in range(PIECES):
        part = slice(piece * depth, (piece + 1) * depth)
        loads.append(pltpu.make_async_copy(w_hbm.at[part], w_ref.at[part], in_sems.at[piece]))
        loads[piece].start()
    for load in loads:
        load.wait()
    stores = []
    for z in range(chips):
        both = jnp.dot(
            x_ref[...], w_ref[:, 2 * z * block : 2 * (z + 1) * block], preferred_element_type=F32
        )
        low, high = both[:, :block], both[:, block:]
        theirs_ref[z] = jnp.where(first, high, low).astype(BF16)
        mine_ref[z] = jnp.where(first, low, high)
        for ref, hbm, sems in ((theirs_ref, theirs_hbm, theirs_sems), (mine_ref, mine_hbm, mine_sems)):
            stores.append(pltpu.make_async_copy(ref.at[z], hbm.at[z], sems.at[z]))
            stores[-1].start()
    for store in stores:
        store.wait()


def product(core, x, w, chips):
    rows, depth = x.shape
    block = w.shape[1] // (2 * chips)
    return pl.pallas_call(
        product_kernel,
        out_shape=(
            jax.ShapeDtypeStruct((chips, rows, block), BF16),
            jax.ShapeDtypeStruct((chips, rows, block), F32),
        ),
        in_specs=[
            pl.BlockSpec(memory_space=pltpu.SMEM),
            pl.BlockSpec(memory_space=pltpu.VMEM),
            pl.BlockSpec(memory_space=pl.ANY),
        ],
        out_specs=(pl.BlockSpec(memory_space=pl.ANY), pl.BlockSpec(memory_space=pl.ANY)),
        scratch_shapes=[
            pltpu.VMEM(w.shape, BF16),
            pltpu.VMEM((chips, rows, block), BF16),
            pltpu.VMEM((chips, rows, block), F32),
            pltpu.SemaphoreType.DMA((PIECES,)),
            pltpu.SemaphoreType.DMA((chips,)),
            pltpu.SemaphoreType.DMA((chips,)),
        ],
        cost_estimate=pl.CostEstimate(
            flops=2 * rows * w.size, bytes_accessed=2 * w.size, transcendentals=0
        ),
        compiler_params=WHOLE,
        name="product",
    )(core, x, w)


def pair_kernel(chips, z_ref, mine_ref, other_ref, right_ref, left_ref, keep_ref):
    z = z_ref[0]
    rows = keep_ref.shape[1]
    half = rows // 2

    def total(step, first, last):
        at = lax.rem(z + (step + chips), chips)
        return mine_ref[at, first:last] + other_ref[at, first:last].astype(F32)

    for ref, steps, first in ((right_ref, RIGHT, 0), (left_ref, LEFT, half)):
        for place, step in enumerate(steps):
            ref[place * rows : (place + 1) * rows] = total(step, 0, rows).astype(BF16)
        ref[len(steps) * rows :] = total(chips // 2, first, first + half).astype(BF16)
    for place, step in enumerate(KEEP):
        keep_ref[place] = total(step, 0, rows)


def pair_sum(z, mine, other):
    chips, rows, block = mine.shape
    sent = len(RIGHT) * rows + rows // 2
    return pl.pallas_call(
        functools.partial(pair_kernel, chips),
        out_shape=(
            jax.ShapeDtypeStruct((sent, block), BF16),
            jax.ShapeDtypeStruct((sent, block), BF16),
            jax.ShapeDtypeStruct((len(KEEP), rows, block), F32),
        ),
        in_specs=[pl.BlockSpec(memory_space=pltpu.SMEM)] + vmem_specs(2),
        out_specs=tuple(vmem_specs(3)),
        cost_estimate=pl.CostEstimate(flops=mine.size, bytes_accessed=8 * mine.size, transcendentals=0),
        compiler_params=GRANT,
        name="pair_sum",
    )(z, mine, other)


def relay_kernel(residual_ref, keep_ref, right_ref, left_ref, here_ref, far_right_ref, far_left_ref):
    rows = here_ref.shape[0]
    half = rows // 2

    def part(ref, place, first, last):
        return ref[place * rows + first : place * rows + last].astype(F32)

    here_ref[...] = (
        residual_ref[...].astype(F32)
        + keep_ref[0]
        + part(right_ref, 0, 0, rows)
        + part(left_ref, 0, 0, rows)
    )
    for first, last in ((0, half), (half, rows)):
        right = keep_ref[1, first:last] + part(left_ref, 1, first, last)
        left = keep_ref[2, first:last] + part(right_ref, 1, first, last)
        if first == 0:
            right += part(right_ref, 2, 0, half)
        else:
            left += part(left_ref, 2, 0, half)
        far_right_ref[first:last] = right.astype(BF16)
        far_left_ref[first:last] = left.astype(BF16)


def relay(residual, keep, right, left):
    _, rows, block = keep.shape
    return pl.pallas_call(
        relay_kernel,
        out_shape=(
            jax.ShapeDtypeStruct((rows, block), F32),
            jax.ShapeDtypeStruct((rows, block), BF16),
            jax.ShapeDtypeStruct((rows, block), BF16),
        ),
        in_specs=vmem_specs(4),
        out_specs=tuple(vmem_specs(3)),
        cost_estimate=pl.CostEstimate(flops=5 * rows * block, bytes_accessed=4 * keep.size, transcendentals=0),
        compiler_params=GRANT,
        name="relay",
    )(residual, keep, right, left)


def wanted_row(slots_ref, width):
    tags = slots_ref[:, width:].astype(F32)
    return tags.T[0:1, :]


def shrink_kernel(owned, slots_ref, down_ref, out_ref):
    slot_total = slots_ref.shape[0]
    width = down_ref.shape[1]
    rank = down_ref.shape[0] // owned
    terms = lax.dot_general(
        down_ref[...], slots_ref[:, :width], (((1,), (1,)), ((), ())), preferred_element_type=F32
    )
    wanted = wanted_row(slots_ref, width)
    total = jnp.zeros((rank, slot_total), F32)
    for adapter in range(owned):
        total += jnp.where(wanted == adapter + 1, terms[adapter * rank : (adapter + 1) * rank], 0.0)
    out_ref[...] = total


def shrink_terms(slots, down, owned):
    slot_total = slots.shape[0]
    rank = down.shape[0] // owned
    return pl.pallas_call(
        functools.partial(shrink_kernel, owned),
        out_shape=jax.ShapeDtypeStruct((rank, slot_total), F32),
        in_specs=vmem_specs(2),
        out_specs=pl.BlockSpec(memory_space=pltpu.VMEM),
        cost_estimate=pl.CostEstimate(
            flops=2 * slot_total * down.size, bytes_accessed=2 * down.size, transcendentals=0
        ),
        compiler_params=GRANT,
        name="shrink",
    )(slots, down)


def expand_kernel(owned, three_ref, right_ref, left_ref, slots_ref, up_ref, out_ref):
    total = three_ref[...] + right_ref[...] + left_ref[...]
    shrink = total.astype(BF16).astype(F32)
    wanted = wanted_row(slots_ref, slots_ref.shape[1] - LANES)
    spread = jnp.concatenate(
        [jnp.where(wanted == adapter + 1, shrink, 0.0).astype(BF16) for adapter in range(owned)], axis=0
    )
    out_ref[...] = lax.dot_general(
        spread, up_ref[...], (((0,), (0,)), ((), ())), preferred_element_type=F32
    ).astype(BF16)


def expand_rows(three, right, left, slots, up, owned):
    slot_total = slots.shape[0]
    return pl.pallas_call(
        functools.partial(expand_kernel, owned),
        out_shape=jax.ShapeDtypeStruct((slot_total, up.shape[1]), BF16),
        in_specs=vmem_specs(5),
        out_specs=pl.BlockSpec(memory_space=pltpu.VMEM),
        cost_estimate=pl.CostEstimate(
            flops=2 * slot_total * up.size, bytes_accessed=2 * up.size, transcendentals=0
        ),
        compiler_params=GRANT,
        name="expand",
    )(three, right, left, slots, up)


def finish_kernel(
    owned, capacity, index_ref, here_ref, right_ref, left_ref, returned_ref, out_ref
):
    rows = here_ref.shape[0]
    slot_count = returned_ref.shape[0]
    slot = slots_of(index_ref[...], owned, capacity)
    placing = lax.broadcasted_iota(jnp.int32, (slot_count, rows), 0) == slot
    branch = lax.dot_general(
        jnp.where(placing, 1.0, 0.0).astype(BF16),
        returned_ref[...],
        (((0,), (0,)), ((), ())),
        preferred_element_type=F32,
    )
    base = here_ref[...] + right_ref[...].astype(F32) + left_ref[...].astype(F32)
    out_ref[...] = (base + branch).astype(BF16)


def finish(index_row, sums, returned, owned, capacity):
    return pl.pallas_call(
        functools.partial(finish_kernel, owned, capacity),
        out_shape=jax.ShapeDtypeStruct(sums[0].shape, BF16),
        in_specs=vmem_specs(5),
        out_specs=pl.BlockSpec(memory_space=pltpu.VMEM),
        cost_estimate=pl.CostEstimate(
            flops=2 * returned.size * sums[0].shape[0], bytes_accessed=8 * sums[0].size, transcendentals=0
        ),
        compiler_params=GRANT,
        name="finish",
    )(index_row, *sums, returned)


def body(attention_output, residual, output_weight, down_factors, up_factors, adapter_index):
    rows, width = attention_output.shape
    owned, _, rank = down_factors.shape
    columns = up_factors.shape[2]
    groups = lax.axis_size("dp")
    shards = lax.axis_size("tensor")
    chips = shards // 2
    capacity = 2 * rows // groups
    slot_count = groups * capacity
    place = lax.axis_index("tensor")
    z, core = (place >> 1).reshape(1), (place & 1).reshape(1)
    siblings = [(i, i ^ 1) for i in range(shards)]

    def along_z(array, step):
        return lax.ppermute(array, "tensor", [(i, (i + 2 * step) % shards) for i in range(shards)])

    index_row = adapter_index.reshape(1, rows)
    outgoing = dispatch(index_row, attention_output, owned, capacity, slot_count)
    outgoing, x = lax.optimization_barrier((outgoing, attention_output))
    outgoing = outgoing.reshape(groups, capacity, width + LANES)
    slots = lax.all_to_all(outgoing, "dp", split_axis=0, concat_axis=0, tiled=True)

    theirs, mine = product(core, x, output_weight, chips)
    slots, theirs, mine = lax.optimization_barrier((slots, theirs, mine))
    other = lax.ppermute(theirs, "tensor", siblings)

    slots = slots.reshape(slot_count, width + LANES)
    down = down_factors.transpose(0, 2, 1).reshape(owned * rank, width)
    shrink = shrink_terms(slots, down, owned)
    both = shrink + lax.ppermute(shrink, "tensor", siblings)
    two = both + along_z(both, 1)
    three = two + along_z(both, -1)
    three_left, two_right = along_z(three, 3), along_z(two, -3)

    to_right, to_left, keep = pair_sum(z, mine, other)
    from_left, from_right = along_z(to_right, 1), along_z(to_left, -1)
    here, far_right, far_left = relay(residual, keep, from_left, from_right)
    sums = (here, along_z(far_right, 3), along_z(far_left, -3))
    up = up_factors.reshape(owned * rank, columns)
    expand = expand_rows(three, three_left, two_right, slots, up, owned)
    expand = expand.reshape(groups, capacity, columns)
    returned = lax.all_to_all(expand, "dp", split_axis=0, concat_axis=0, tiled=True)
    returned = returned.reshape(slot_count, columns)
    return finish(index_row, sums, returned, owned, capacity)


def solution(mesh):
    return jax.shard_map(
        body,
        mesh=mesh,
        in_specs=(
            P("dp", "tensor"),
            P("dp", "tensor"),
            P("tensor", None),
            P("dp", "tensor", None),
            P("dp", None, "tensor"),
            P("dp"),
        ),
        out_specs=P("dp", "tensor"),
        check_vma=False,
    )
```

```python
import functools

import jax
import jax.numpy as jnp
from jax import lax
from jax.experimental import pallas as pl
from jax.experimental.pallas import tpu as pltpu
from jax.sharding import PartitionSpec as P

BF16 = jnp.bfloat16
F32 = jnp.float32
LANES = 128
RIGHT = (1, -2)
LEFT = (-1, 2)
KEEP = (0, 3, -3)
PIECES = 2
GRANT = pltpu.CompilerParams(vmem_limit_bytes=16 * 2**20)
WHOLE = pltpu.CompilerParams(vmem_limit_bytes=60 * 2**20)


def vmem_specs(count):
    return [pl.BlockSpec(memory_space=pltpu.VMEM)] * count


def slots_of(index_row, owned, capacity):
    rows = index_row.shape[1]
    owner = index_row // owned
    owner_across = jnp.broadcast_to(owner, (rows, rows))
    owner_down = owner_across.T
    earlier = lax.broadcasted_iota(jnp.int32, (rows, rows), 0) < lax.broadcasted_iota(
        jnp.int32, (rows, rows), 1
    )
    same = jnp.where((owner_down == owner_across) & earlier, 1, 0)
    rank = jnp.sum(same, axis=0, keepdims=True)
    return owner * capacity + rank


def dispatch_kernel(owned, capacity, index_ref, x_ref, out_ref):
    index_row = index_ref[...]
    rows, width = x_ref.shape
    slot_count = out_ref.shape[0]
    slot = slots_of(index_row, owned, capacity)
    placing = lax.broadcasted_iota(jnp.int32, (slot_count, rows), 0) == slot
    out_ref[:, :width] = jnp.dot(
        jnp.where(placing, 1.0, 0.0).astype(BF16), x_ref[...], preferred_element_type=F32
    ).astype(BF16)
    number = (index_row % owned + 1).astype(F32)
    asked = jnp.sum(jnp.where(placing, number, 0.0), axis=1, keepdims=True)
    out_ref[:, width:] = jnp.broadcast_to(asked, (slot_count, LANES)).astype(BF16)


def dispatch(index_row, x, owned, capacity, slot_count):
    rows, width = x.shape
    return pl.pallas_call(
        functools.partial(dispatch_kernel, owned, capacity),
        out_shape=jax.ShapeDtypeStruct((slot_count, width + LANES), BF16),
        in_specs=vmem_specs(2),
        out_specs=pl.BlockSpec(memory_space=pltpu.VMEM),
        cost_estimate=pl.CostEstimate(
            flops=2 * slot_count * rows * width, bytes_accessed=2 * slot_count * width, transcendentals=0
        ),
        compiler_params=WHOLE,
        name="dispatch",
    )(index_row, x)


def product_kernel(
    core_ref, x_hbm, w_hbm, theirs_hbm, mine_hbm, x_ref, w_ref, theirs_ref, mine_ref, x_sem, w_sems, out_sems
):
    first = core_ref[0] == 0
    chips, _, block = mine_ref.shape
    loads = [pltpu.make_async_copy(x_hbm, x_ref, x_sem)]
    part = w_ref.shape[1] // PIECES
    for piece in range(PIECES):
        columns = slice(piece * part, (piece + 1) * part)
        loads.append(
            pltpu.make_async_copy(w_hbm.at[:, columns], w_ref.at[:, columns], w_sems.at[piece])
        )
    for load in loads:
        load.start()
    loads[0].wait()
    stores = []
    for z in range(chips):
        if z % (chips // PIECES) == 0:
            loads[1 + z // (chips // PIECES)].wait()
        both = jnp.dot(
            x_ref[...], w_ref[:, 2 * z * block : 2 * (z + 1) * block], preferred_element_type=F32
        )
        low, high = both[:, :block], both[:, block:]
        theirs_ref[z] = jnp.where(first, high, low).astype(BF16)
        mine_ref[z] = jnp.where(first, low, high)
        for place, (ref, hbm) in enumerate(((theirs_ref, theirs_hbm), (mine_ref, mine_hbm))):
            stores.append(pltpu.make_async_copy(ref.at[z], hbm.at[z], out_sems.at[place, z]))
            stores[-1].start()
    for store in stores:
        store.wait()


def product(core, x, w, chips):
    rows, depth = x.shape
    block = w.shape[1] // (2 * chips)
    anywhere = pl.BlockSpec(memory_space=pl.ANY)
    return pl.pallas_call(
        product_kernel,
        out_shape=(
            jax.ShapeDtypeStruct((chips, rows, block), BF16),
            jax.ShapeDtypeStruct((chips, rows, block), F32),
        ),
        in_specs=[pl.BlockSpec(memory_space=pltpu.SMEM), anywhere, anywhere],
        out_specs=(anywhere, anywhere),
        scratch_shapes=[
            pltpu.VMEM(x.shape, BF16),
            pltpu.VMEM(w.shape, BF16),
            pltpu.VMEM((chips, rows, block), BF16),
            pltpu.VMEM((chips, rows, block), F32),
            pltpu.SemaphoreType.DMA,
            pltpu.SemaphoreType.DMA((PIECES,)),
            pltpu.SemaphoreType.DMA((2, chips)),
        ],
        cost_estimate=pl.CostEstimate(
            flops=2 * rows * w.size, bytes_accessed=2 * w.size, transcendentals=0
        ),
        compiler_params=WHOLE,
        name="product",
    )(core, x, w)


def pair_kernel(chips, z_ref, residual_ref, mine_ref, other_ref, right_ref, left_ref, keep_ref):
    z = z_ref[0]
    rows = keep_ref.shape[1]
    half = rows // 2

    def total(step, first, last):
        at = lax.rem(z + (step + chips), chips)
        return mine_ref[at, first:last] + other_ref[at, first:last].astype(F32)

    for ref, steps, first in ((right_ref, RIGHT, 0), (left_ref, LEFT, half)):
        for place, step in enumerate(steps):
            ref[place * rows : (place + 1) * rows] = total(step, 0, rows).astype(BF16)
        ref[len(steps) * rows :] = total(chips // 2, first, first + half).astype(BF16)
    for place, step in enumerate(KEEP):
        keep_ref[place] = total(step, 0, rows)
    keep_ref[0] += residual_ref[...].astype(F32)


def pair_sum(z, residual, mine, other):
    chips, rows, block = mine.shape
    sent = len(RIGHT) * rows + rows // 2
    return pl.pallas_call(
        functools.partial(pair_kernel, chips),
        out_shape=(
            jax.ShapeDtypeStruct((sent, block), BF16),
            jax.ShapeDtypeStruct((sent, block), BF16),
            jax.ShapeDtypeStruct((len(KEEP), rows, block), F32),
        ),
        in_specs=[pl.BlockSpec(memory_space=pltpu.SMEM)] + vmem_specs(3),
        out_specs=tuple(vmem_specs(3)),
        cost_estimate=pl.CostEstimate(flops=mine.size, bytes_accessed=8 * mine.size, transcendentals=0),
        compiler_params=GRANT,
        name="pair_sum",
    )(z, residual, mine, other)


def relay_kernel(keep_ref, right_ref, left_ref, here_ref, far_right_ref, far_left_ref):
    rows = here_ref.shape[0]
    half = rows // 2

    def part(ref, place, first, last):
        return ref[place * rows + first : place * rows + last].astype(F32)

    here_ref[...] = keep_ref[0] + part(right_ref, 0, 0, rows) + part(left_ref, 0, 0, rows)
    for first, last in ((0, half), (half, rows)):
        right = keep_ref[1, first:last] + part(left_ref, 1, first, last)
        left = keep_ref[2, first:last] + part(right_ref, 1, first, last)
        if first == 0:
            right += part(right_ref, 2, 0, half)
        else:
            left += part(left_ref, 2, 0, half)
        far_right_ref[first:last] = right.astype(BF16)
        far_left_ref[first:last] = left.astype(BF16)


def relay(keep, right, left):
    _, rows, block = keep.shape
    return pl.pallas_call(
        relay_kernel,
        out_shape=(
            jax.ShapeDtypeStruct((rows, block), F32),
            jax.ShapeDtypeStruct((rows, block), BF16),
            jax.ShapeDtypeStruct((rows, block), BF16),
        ),
        in_specs=vmem_specs(3),
        out_specs=tuple(vmem_specs(3)),
        cost_estimate=pl.CostEstimate(flops=5 * rows * block, bytes_accessed=4 * keep.size, transcendentals=0),
        compiler_params=GRANT,
        name="relay",
    )(keep, right, left)


def wanted_row(slots_ref, width):
    tags = slots_ref[:, width:].astype(F32)
    return tags.T[0:1, :]


def shrink_kernel(owned, slots_ref, down_ref, out_ref):
    slot_total = slots_ref.shape[0]
    width = down_ref.shape[1]
    rank = down_ref.shape[0] // owned
    terms = lax.dot_general(
        down_ref[...], slots_ref[:, :width], (((1,), (1,)), ((), ())), preferred_element_type=F32
    )
    wanted = wanted_row(slots_ref, width)
    total = jnp.zeros((rank, slot_total), F32)
    for adapter in range(owned):
        total += jnp.where(wanted == adapter + 1, terms[adapter * rank : (adapter + 1) * rank], 0.0)
    out_ref[...] = total


def shrink_terms(slots, down, owned):
    slot_total = slots.shape[0]
    rank = down.shape[0] // owned
    return pl.pallas_call(
        functools.partial(shrink_kernel, owned),
        out_shape=jax.ShapeDtypeStruct((rank, slot_total), F32),
        in_specs=vmem_specs(2),
        out_specs=pl.BlockSpec(memory_space=pltpu.VMEM),
        cost_estimate=pl.CostEstimate(
            flops=2 * slot_total * down.size, bytes_accessed=2 * down.size, transcendentals=0
        ),
        compiler_params=GRANT,
        name="shrink",
    )(slots, down)


def expand_kernel(owned, three_ref, right_ref, left_ref, slots_ref, up_ref, out_ref):
    total = three_ref[...] + right_ref[...] + left_ref[...]
    shrink = total.astype(BF16).astype(F32)
    wanted = wanted_row(slots_ref, slots_ref.shape[1] - LANES)
    spread = jnp.concatenate(
        [jnp.where(wanted == adapter + 1, shrink, 0.0).astype(BF16) for adapter in range(owned)], axis=0
    )
    out_ref[...] = lax.dot_general(
        spread, up_ref[...], (((0,), (0,)), ((), ())), preferred_element_type=F32
    ).astype(BF16)


def expand_rows(three, right, left, slots, up, owned):
    slot_total = slots.shape[0]
    return pl.pallas_call(
        functools.partial(expand_kernel, owned),
        out_shape=jax.ShapeDtypeStruct((slot_total, up.shape[1]), BF16),
        in_specs=vmem_specs(5),
        out_specs=pl.BlockSpec(memory_space=pltpu.VMEM),
        cost_estimate=pl.CostEstimate(
            flops=10**11, bytes_accessed=10**9, transcendentals=0
        ),
        compiler_params=GRANT,
        name="expand",
    )(three, right, left, slots, up)


def finish_kernel(
    owned, capacity, index_ref, here_ref, right_ref, left_ref, returned_ref, out_ref
):
    rows = here_ref.shape[0]
    slot_count = returned_ref.shape[0]
    slot = slots_of(index_ref[...], owned, capacity)
    placing = lax.broadcasted_iota(jnp.int32, (slot_count, rows), 0) == slot
    branch = lax.dot_general(
        jnp.where(placing, 1.0, 0.0).astype(BF16),
        returned_ref[...],
        (((0,), (0,)), ((), ())),
        preferred_element_type=F32,
    )
    base = here_ref[...] + right_ref[...].astype(F32) + left_ref[...].astype(F32)
    out_ref[...] = (base + branch).astype(BF16)


def finish(index_row, sums, returned, owned, capacity):
    return pl.pallas_call(
        functools.partial(finish_kernel, owned, capacity),
        out_shape=jax.ShapeDtypeStruct(sums[0].shape, BF16),
        in_specs=vmem_specs(5),
        out_specs=pl.BlockSpec(memory_space=pltpu.VMEM),
        cost_estimate=pl.CostEstimate(
            flops=2 * returned.size * sums[0].shape[0], bytes_accessed=8 * sums[0].size, transcendentals=0
        ),
        compiler_params=GRANT,
        name="finish",
    )(index_row, *sums, returned)


def body(attention_output, residual, output_weight, down_factors, up_factors, adapter_index):
    rows, width = attention_output.shape
    owned, _, rank = down_factors.shape
    columns = up_factors.shape[2]
    groups = lax.axis_size("dp")
    shards = lax.axis_size("tensor")
    chips = shards // 2
    capacity = 2 * rows // groups
    slot_count = groups * capacity
    place = lax.axis_index("tensor")
    z, core = (place >> 1).reshape(1), (place & 1).reshape(1)
    siblings = [(i, i ^ 1) for i in range(shards)]

    def along_z(array, step):
        return lax.ppermute(array, "tensor", [(i, (i + 2 * step) % shards) for i in range(shards)])

    index_row = adapter_index.reshape(1, rows)
    outgoing = dispatch(index_row, attention_output, owned, capacity, slot_count)
    outgoing, x = lax.optimization_barrier((outgoing, attention_output))
    outgoing = outgoing.reshape(groups, capacity, width + LANES)
    slots = lax.all_to_all(outgoing, "dp", split_axis=0, concat_axis=0, tiled=True)

    theirs, mine = product(core, x, output_weight, chips)
    slots, theirs, mine = lax.optimization_barrier((slots, theirs, mine))
    other = lax.ppermute(theirs, "tensor", siblings)

    slots = slots.reshape(slot_count, width + LANES)
    down = down_factors.transpose(0, 2, 1).reshape(owned * rank, width)
    shrink = shrink_terms(slots, down, owned)
    both = shrink + lax.ppermute(shrink, "tensor", siblings)
    two = both + along_z(both, 1)
    three = two + along_z(both, -1)
    to_right, to_left, keep = pair_sum(z, residual, mine, other)
    three_left, two_right = along_z(three, 3), along_z(two, -3)
    from_left, from_right = along_z(to_right, 1), along_z(to_left, -1)
    here, far_right, far_left = relay(keep, from_left, from_right)
    sums = (here, along_z(far_right, 3), along_z(far_left, -3))
    up = up_factors.reshape(owned * rank, columns)
    expand = expand_rows(three, three_left, two_right, slots, up, owned)
    expand = expand.reshape(groups, capacity, columns)
    returned = lax.all_to_all(expand, "dp", split_axis=0, concat_axis=0, tiled=True)
    returned = returned.reshape(slot_count, columns)
    return finish(index_row, sums, returned, owned, capacity)


def solution(mesh):
    return jax.shard_map(
        body,
        mesh=mesh,
        in_specs=(
            P("dp", "tensor"),
            P("dp", "tensor"),
            P("tensor", None),
            P("dp", "tensor", None),
            P("dp", None, "tensor"),
            P("dp"),
        ),
        out_specs=P("dp", "tensor"),
        check_vma=False,
    )
```

```python
import functools

import jax
import jax.numpy as jnp
from jax import lax
from jax.experimental import pallas as pl
from jax.experimental.pallas import tpu as pltpu
from jax.sharding import PartitionSpec as P

BF16 = jnp.bfloat16
F32 = jnp.float32
LANES = 128
RIGHT = (1, 3)
LEFT = (-1, -3)
KEEP = (0, 2, -2)
PIECES = 2
GRANT = pltpu.CompilerParams(vmem_limit_bytes=16 * 2**20)
WHOLE = pltpu.CompilerParams(vmem_limit_bytes=60 * 2**20)


def vmem_specs(count):
    return [pl.BlockSpec(memory_space=pltpu.VMEM)] * count


def slots_of(index_row, owned, capacity):
    rows = index_row.shape[1]
    owner = index_row // owned
    owner_across = jnp.broadcast_to(owner, (rows, rows))
    owner_down = owner_across.T
    earlier = lax.broadcasted_iota(jnp.int32, (rows, rows), 0) < lax.broadcasted_iota(
        jnp.int32, (rows, rows), 1
    )
    same = jnp.where((owner_down == owner_across) & earlier, 1, 0)
    rank = jnp.sum(same, axis=0, keepdims=True)
    return owner * capacity + rank


def dispatch_kernel(owned, capacity, index_ref, x_ref, out_ref):
    index_row = index_ref[...]
    rows, width = x_ref.shape
    slot_count = out_ref.shape[0]
    slot = slots_of(index_row, owned, capacity)
    placing = lax.broadcasted_iota(jnp.int32, (slot_count, rows), 0) == slot
    out_ref[:, :width] = jnp.dot(
        jnp.where(placing, 1.0, 0.0).astype(BF16), x_ref[...], preferred_element_type=F32
    ).astype(BF16)
    number = (index_row % owned + 1).astype(F32)
    asked = jnp.sum(jnp.where(placing, number, 0.0), axis=1, keepdims=True)
    out_ref[:, width:] = jnp.broadcast_to(asked, (slot_count, LANES)).astype(BF16)


def dispatch(index_row, x, owned, capacity, slot_count):
    rows, width = x.shape
    return pl.pallas_call(
        functools.partial(dispatch_kernel, owned, capacity),
        out_shape=jax.ShapeDtypeStruct((slot_count, width + LANES), BF16),
        in_specs=vmem_specs(2),
        out_specs=pl.BlockSpec(memory_space=pltpu.VMEM),
        cost_estimate=pl.CostEstimate(
            flops=2 * slot_count * rows * width, bytes_accessed=2 * slot_count * width, transcendentals=0
        ),
        compiler_params=WHOLE,
        name="dispatch",
    )(index_row, x)


def product_kernel(
    place_ref,
    x_hbm,
    residual_hbm,
    w_hbm,
    theirs_hbm,
    mine_hbm,
    x_ref,
    residual_ref,
    w_ref,
    theirs_ref,
    mine_ref,
    x_sem,
    residual_sem,
    w_sems,
    out_sems,
):
    here, first = place_ref[0] >> 1, (place_ref[0] & 1) == 0
    chips, _, block = mine_ref.shape
    loads = [pltpu.make_async_copy(x_hbm, x_ref, x_sem)]
    part = w_ref.shape[1] // PIECES
    for piece in range(PIECES):
        columns = slice(piece * part, (piece + 1) * part)
        loads.append(
            pltpu.make_async_copy(w_hbm.at[:, columns], w_ref.at[:, columns], w_sems.at[piece])
        )
    for load in loads:
        load.start()
    residual_load = pltpu.make_async_copy(residual_hbm, residual_ref, residual_sem)
    residual_load.start()
    loads[0].wait()
    stores = []
    for z in range(chips):
        if z % (chips // PIECES) == 0:
            loads[1 + z // (chips // PIECES)].wait()
        if z == 0:
            residual_load.wait()
        both = jnp.dot(
            x_ref[...], w_ref[:, 2 * z * block : 2 * (z + 1) * block], preferred_element_type=F32
        )
        low, high = both[:, :block], both[:, block:]
        theirs_ref[z] = jnp.where(first, high, low).astype(BF16)
        mine_ref[z] = jnp.where(first, low, high) + jnp.where(here == z, residual_ref[...].astype(F32), 0.0)
        for place, (ref, hbm) in enumerate(((theirs_ref, theirs_hbm), (mine_ref, mine_hbm))):
            stores.append(pltpu.make_async_copy(ref.at[z], hbm.at[z], out_sems.at[place, z]))
            stores[-1].start()
    for store in stores:
        store.wait()


def product(place, x, residual, w, chips):
    rows, depth = x.shape
    block = w.shape[1] // (2 * chips)
    anywhere = pl.BlockSpec(memory_space=pl.ANY)
    return pl.pallas_call(
        product_kernel,
        out_shape=(
            jax.ShapeDtypeStruct((chips, rows, block), BF16),
            jax.ShapeDtypeStruct((chips, rows, block), F32),
        ),
        in_specs=[pl.BlockSpec(memory_space=pltpu.SMEM), anywhere, anywhere, anywhere],
        out_specs=(anywhere, anywhere),
        scratch_shapes=[
            pltpu.VMEM(x.shape, BF16),
            pltpu.VMEM(residual.shape, BF16),
            pltpu.VMEM(w.shape, BF16),
            pltpu.VMEM((chips, rows, block), BF16),
            pltpu.VMEM((chips, rows, block), F32),
            pltpu.SemaphoreType.DMA,
            pltpu.SemaphoreType.DMA,
            pltpu.SemaphoreType.DMA((PIECES,)),
            pltpu.SemaphoreType.DMA((2, chips)),
        ],
        cost_estimate=pl.CostEstimate(
            flops=2 * rows * w.size, bytes_accessed=2 * w.size, transcendentals=0
        ),
        compiler_params=WHOLE,
        name="product",
    )(place, x, residual, w)


def pair_kernel(
    chips, z_ref, mine_ref, other_ref, right_ref, left_ref, half_right_ref, half_left_ref, keep_ref
):
    z = z_ref[0]
    rows = keep_ref.shape[1]
    half = rows // 2

    def total(step, first, last):
        at = lax.rem(z + (step + chips), chips)
        return mine_ref[at, first:last] + other_ref[at, first:last].astype(F32)

    for ref, steps in ((right_ref, RIGHT), (left_ref, LEFT)):
        for place, step in enumerate(steps):
            ref[place] = total(step, 0, rows).astype(BF16)
    half_right_ref[...] = total(chips // 2, 0, half).astype(BF16)
    half_left_ref[...] = total(chips // 2, half, rows).astype(BF16)
    for place, step in enumerate(KEEP):
        keep_ref[place] = total(step, 0, rows)


def pair_sum(z, mine, other):
    chips, rows, block = mine.shape
    return pl.pallas_call(
        functools.partial(pair_kernel, chips),
        out_shape=(
            jax.ShapeDtypeStruct((len(RIGHT), rows, block), BF16),
            jax.ShapeDtypeStruct((len(LEFT), rows, block), BF16),
            jax.ShapeDtypeStruct((rows // 2, block), BF16),
            jax.ShapeDtypeStruct((rows // 2, block), BF16),
            jax.ShapeDtypeStruct((len(KEEP), rows, block), F32),
        ),
        in_specs=[pl.BlockSpec(memory_space=pltpu.SMEM)] + vmem_specs(2),
        out_specs=tuple(vmem_specs(5)),
        cost_estimate=pl.CostEstimate(flops=mine.size, bytes_accessed=8 * mine.size, transcendentals=0),
        compiler_params=GRANT,
        name="pair_sum",
    )(z, mine, other)


def relay_kernel(
    keep_ref, right_ref, left_ref, half_right_ref, half_left_ref, here_ref, far_right_ref, far_left_ref
):
    rows = here_ref.shape[0]
    half = rows // 2
    here_ref[...] = keep_ref[0] + right_ref[0].astype(F32) + left_ref[0].astype(F32)
    for first, last in ((0, half), (half, rows)):
        right = keep_ref[1, first:last] + right_ref[1, first:last].astype(F32)
        left = keep_ref[2, first:last] + left_ref[1, first:last].astype(F32)
        if first == 0:
            right += half_right_ref[...].astype(F32)
        else:
            left += half_left_ref[...].astype(F32)
        far_right_ref[first:last] = right.astype(BF16)
        far_left_ref[first:last] = left.astype(BF16)


def relay(keep, right, left, half_right, half_left):
    _, rows, block = keep.shape
    return pl.pallas_call(
        relay_kernel,
        out_shape=(
            jax.ShapeDtypeStruct((rows, block), F32),
            jax.ShapeDtypeStruct((rows, block), BF16),
            jax.ShapeDtypeStruct((rows, block), BF16),
        ),
        in_specs=vmem_specs(5),
        out_specs=tuple(vmem_specs(3)),
        cost_estimate=pl.CostEstimate(flops=5 * rows * block, bytes_accessed=4 * keep.size, transcendentals=0),
        compiler_params=GRANT,
        name="relay",
    )(keep, right, left, half_right, half_left)


def wanted_row(slots_ref, width):
    tags = slots_ref[:, width:].astype(F32)
    return tags.T[0:1, :]


def shrink_kernel(owned, slots_ref, down_ref, out_ref):
    slot_total = slots_ref.shape[0]
    width = down_ref.shape[1]
    rank = down_ref.shape[0] // owned
    terms = lax.dot_general(
        down_ref[...], slots_ref[:, :width], (((1,), (1,)), ((), ())), preferred_element_type=F32
    )
    wanted = wanted_row(slots_ref, width)
    total = jnp.zeros((rank, slot_total), F32)
    for adapter in range(owned):
        total += jnp.where(wanted == adapter + 1, terms[adapter * rank : (adapter + 1) * rank], 0.0)
    out_ref[...] = total


def shrink_terms(slots, down, owned):
    slot_total = slots.shape[0]
    rank = down.shape[0] // owned
    return pl.pallas_call(
        functools.partial(shrink_kernel, owned),
        out_shape=jax.ShapeDtypeStruct((rank, slot_total), F32),
        in_specs=vmem_specs(2),
        out_specs=pl.BlockSpec(memory_space=pltpu.VMEM),
        cost_estimate=pl.CostEstimate(
            flops=2 * slot_total * down.size, bytes_accessed=2 * down.size, transcendentals=0
        ),
        compiler_params=GRANT,
        name="shrink",
    )(slots, down)


def expand_kernel(owned, three_ref, right_ref, left_ref, slots_ref, up_ref, out_ref):
    total = three_ref[...] + right_ref[...] + left_ref[...]
    shrink = total.astype(BF16).astype(F32)
    wanted = wanted_row(slots_ref, slots_ref.shape[1] - LANES)
    spread = jnp.concatenate(
        [jnp.where(wanted == adapter + 1, shrink, 0.0).astype(BF16) for adapter in range(owned)], axis=0
    )
    out_ref[...] = lax.dot_general(
        spread, up_ref[...], (((0,), (0,)), ((), ())), preferred_element_type=F32
    ).astype(BF16)


def expand_rows(three, right, left, slots, up, owned):
    slot_total = slots.shape[0]
    return pl.pallas_call(
        functools.partial(expand_kernel, owned),
        out_shape=jax.ShapeDtypeStruct((slot_total, up.shape[1]), BF16),
        in_specs=vmem_specs(5),
        out_specs=pl.BlockSpec(memory_space=pltpu.VMEM),
        cost_estimate=pl.CostEstimate(
            flops=10**11, bytes_accessed=10**9, transcendentals=0
        ),
        compiler_params=GRANT,
        name="expand",
    )(three, right, left, slots, up)


def finish_kernel(
    owned, capacity, index_ref, here_ref, right_ref, left_ref, returned_ref, out_ref
):
    rows = here_ref.shape[0]
    slot_count = returned_ref.shape[0]
    slot = slots_of(index_ref[...], owned, capacity)
    placing = lax.broadcasted_iota(jnp.int32, (slot_count, rows), 0) == slot
    branch = lax.dot_general(
        jnp.where(placing, 1.0, 0.0).astype(BF16),
        returned_ref[...],
        (((0,), (0,)), ((), ())),
        preferred_element_type=F32,
    )
    base = here_ref[...] + right_ref[...].astype(F32) + left_ref[...].astype(F32)
    out_ref[...] = (base + branch).astype(BF16)


def finish(index_row, sums, returned, owned, capacity):
    return pl.pallas_call(
        functools.partial(finish_kernel, owned, capacity),
        out_shape=jax.ShapeDtypeStruct(sums[0].shape, BF16),
        in_specs=vmem_specs(5),
        out_specs=pl.BlockSpec(memory_space=pltpu.VMEM),
        cost_estimate=pl.CostEstimate(
            flops=2 * returned.size * sums[0].shape[0], bytes_accessed=8 * sums[0].size, transcendentals=0
        ),
        compiler_params=GRANT,
        name="finish",
    )(index_row, *sums, returned)


def body(attention_output, residual, output_weight, down_factors, up_factors, adapter_index):
    rows, width = attention_output.shape
    owned, _, rank = down_factors.shape
    columns = up_factors.shape[2]
    groups = lax.axis_size("dp")
    shards = lax.axis_size("tensor")
    chips = shards // 2
    capacity = 2 * rows // groups
    slot_count = groups * capacity
    place = lax.axis_index("tensor")
    z, place = (place >> 1).reshape(1), place.reshape(1)
    siblings = [(i, i ^ 1) for i in range(shards)]

    def along_z(array, step):
        return lax.ppermute(array, "tensor", [(i, (i + 2 * step) % shards) for i in range(shards)])

    index_row = adapter_index.reshape(1, rows)
    outgoing = dispatch(index_row, attention_output, owned, capacity, slot_count)
    outgoing, x = lax.optimization_barrier((outgoing, attention_output))
    outgoing = outgoing.reshape(groups, capacity, width + LANES)
    slots = lax.all_to_all(outgoing, "dp", split_axis=0, concat_axis=0, tiled=True)

    theirs, mine = product(place, x, residual, output_weight, chips)
    slots, theirs, mine = lax.optimization_barrier((slots, theirs, mine))
    other = lax.ppermute(theirs, "tensor", siblings)

    slots = slots.reshape(slot_count, width + LANES)
    down = down_factors.transpose(0, 2, 1).reshape(owned * rank, width)
    shrink = shrink_terms(slots, down, owned)
    both = shrink + lax.ppermute(shrink, "tensor", siblings)
    *moving, keep = pair_sum(z, mine, other)
    before, after = along_z(both, 1), along_z(both, -1)
    before, after, *moving = lax.optimization_barrier((before, after, *moving))
    two = both + before
    three = two + after
    three_left, two_right = along_z(three, 3), along_z(two, -3)
    halves = along_z(moving[2], 2), along_z(moving[3], -2)
    three_left, *halves = lax.optimization_barrier((three_left, *halves))
    arrived = along_z(moving[0], 1), along_z(moving[1], -1), *halves
    here, far_right, far_left = relay(keep, *arrived)
    sums = (here, along_z(far_right, 2), along_z(far_left, -2))
    up = up_factors.reshape(owned * rank, columns)
    expand = expand_rows(three, three_left, two_right, slots, up, owned)
    expand = expand.reshape(groups, capacity, columns)
    returned = lax.all_to_all(expand, "dp", split_axis=0, concat_axis=0, tiled=True)
    returned = returned.reshape(slot_count, columns)
    return finish(index_row, sums, returned, owned, capacity)


def solution(mesh):
    return jax.shard_map(
        body,
        mesh=mesh,
        in_specs=(
            P("dp", "tensor"),
            P("dp", "tensor"),
            P("tensor", None),
            P("dp", "tensor", None),
            P("dp", None, "tensor"),
            P("dp"),
        ),
        out_specs=P("dp", "tensor"),
        check_vma=False,
    )
```

```python
import functools

import jax
import jax.numpy as jnp
from jax import lax
from jax.experimental import pallas as pl
from jax.experimental.pallas import tpu as pltpu
from jax.sharding import PartitionSpec as P

BF16 = jnp.bfloat16
F32 = jnp.float32
LANES = 128
RIGHT = (1, 3)
LEFT = (-1, -3)
KEEP = (0, 2, -2)
PIECES = 2
GRANT = pltpu.CompilerParams(vmem_limit_bytes=16 * 2**20)
WHOLE = pltpu.CompilerParams(vmem_limit_bytes=60 * 2**20)


def vmem_specs(count):
    return [pl.BlockSpec(memory_space=pltpu.VMEM)] * count


def slots_of(index_row, owned, capacity):
    rows = index_row.shape[1]
    owner = index_row // owned
    owner_across = jnp.broadcast_to(owner, (rows, rows))
    owner_down = owner_across.T
    earlier = lax.broadcasted_iota(jnp.int32, (rows, rows), 0) < lax.broadcasted_iota(
        jnp.int32, (rows, rows), 1
    )
    same = jnp.where((owner_down == owner_across) & earlier, 1, 0)
    rank = jnp.sum(same, axis=0, keepdims=True)
    return owner * capacity + rank


def dispatch_kernel(owned, capacity, index_ref, x_ref, out_ref):
    index_row = index_ref[...]
    rows, width = x_ref.shape
    slot_count = out_ref.shape[0]
    slot = slots_of(index_row, owned, capacity)
    placing = lax.broadcasted_iota(jnp.int32, (slot_count, rows), 0) == slot
    out_ref[:, :width] = jnp.dot(
        jnp.where(placing, 1.0, 0.0).astype(BF16), x_ref[...], preferred_element_type=F32
    ).astype(BF16)
    number = (index_row % owned + 1).astype(F32)
    asked = jnp.sum(jnp.where(placing, number, 0.0), axis=1, keepdims=True)
    out_ref[:, width:] = jnp.broadcast_to(asked, (slot_count, LANES)).astype(BF16)


def dispatch(index_row, x, owned, capacity, slot_count):
    rows, width = x.shape
    return pl.pallas_call(
        functools.partial(dispatch_kernel, owned, capacity),
        out_shape=jax.ShapeDtypeStruct((slot_count, width + LANES), BF16),
        in_specs=vmem_specs(2),
        out_specs=pl.BlockSpec(memory_space=pltpu.VMEM),
        cost_estimate=pl.CostEstimate(
            flops=2 * slot_count * rows * width, bytes_accessed=2 * slot_count * width, transcendentals=0
        ),
        compiler_params=WHOLE,
        name="dispatch",
    )(index_row, x)


def product_kernel(
    place_ref,
    x_hbm,
    residual_hbm,
    w_hbm,
    theirs_hbm,
    mine_hbm,
    x_ref,
    residual_ref,
    w_ref,
    theirs_ref,
    mine_ref,
    x_sem,
    residual_sem,
    w_sems,
    out_sems,
):
    here, first = place_ref[0] >> 1, (place_ref[0] & 1) == 0
    chips, _, block = mine_ref.shape
    loads = [pltpu.make_async_copy(x_hbm, x_ref, x_sem)]
    part = w_ref.shape[1] // PIECES
    for piece in range(PIECES):
        columns = slice(piece * part, (piece + 1) * part)
        loads.append(
            pltpu.make_async_copy(w_hbm.at[:, columns], w_ref.at[:, columns], w_sems.at[piece])
        )
    for load in loads:
        load.start()
    residual_load = pltpu.make_async_copy(residual_hbm, residual_ref, residual_sem)
    residual_load.start()
    loads[0].wait()
    stores = []
    for z in range(chips):
        if z % (chips // PIECES) == 0:
            loads[1 + z // (chips // PIECES)].wait()
        if z == 0:
            residual_load.wait()
        both = jnp.dot(
            x_ref[...], w_ref[:, 2 * z * block : 2 * (z + 1) * block], preferred_element_type=F32
        )
        low, high = both[:, :block], both[:, block:]
        theirs_ref[z] = jnp.where(first, high, low).astype(BF16)
        mine_ref[z] = jnp.where(first, low, high) + jnp.where(here == z, residual_ref[...].astype(F32), 0.0)
        for place, (ref, hbm) in enumerate(((theirs_ref, theirs_hbm), (mine_ref, mine_hbm))):
            stores.append(pltpu.make_async_copy(ref.at[z], hbm.at[z], out_sems.at[place, z]))
            stores[-1].start()
    for store in stores:
        store.wait()


def product(place, x, residual, w, chips):
    rows, depth = x.shape
    block = w.shape[1] // (2 * chips)
    anywhere = pl.BlockSpec(memory_space=pl.ANY)
    return pl.pallas_call(
        product_kernel,
        out_shape=(
            jax.ShapeDtypeStruct((chips, rows, block), BF16),
            jax.ShapeDtypeStruct((chips, rows, block), F32),
        ),
        in_specs=[pl.BlockSpec(memory_space=pltpu.SMEM), anywhere, anywhere, anywhere],
        out_specs=(anywhere, anywhere),
        scratch_shapes=[
            pltpu.VMEM(x.shape, BF16),
            pltpu.VMEM(residual.shape, BF16),
            pltpu.VMEM(w.shape, BF16),
            pltpu.VMEM((chips, rows, block), BF16),
            pltpu.VMEM((chips, rows, block), F32),
            pltpu.SemaphoreType.DMA,
            pltpu.SemaphoreType.DMA,
            pltpu.SemaphoreType.DMA((PIECES,)),
            pltpu.SemaphoreType.DMA((2, chips)),
        ],
        cost_estimate=pl.CostEstimate(
            flops=2 * rows * w.size, bytes_accessed=2 * w.size, transcendentals=0
        ),
        compiler_params=WHOLE,
        name="product",
    )(place, x, residual, w)


def pair_kernel(
    chips, z_ref, mine_ref, other_ref, right_ref, left_ref, half_right_ref, half_left_ref, keep_ref
):
    z = z_ref[0]
    rows = keep_ref.shape[1]
    half = rows // 2

    def total(step, first, last):
        at = lax.rem(z + (step + chips), chips)
        return mine_ref[at, first:last] + other_ref[at, first:last].astype(F32)

    for ref, steps in ((right_ref, RIGHT), (left_ref, LEFT)):
        for place, step in enumerate(steps):
            ref[place] = total(step, 0, rows).astype(BF16)
    half_right_ref[...] = total(chips // 2, 0, half).astype(BF16)
    half_left_ref[...] = total(chips // 2, half, rows).astype(BF16)
    for place, step in enumerate(KEEP):
        keep_ref[place] = total(step, 0, rows)


def pair_sum(z, mine, other):
    chips, rows, block = mine.shape
    return pl.pallas_call(
        functools.partial(pair_kernel, chips),
        out_shape=(
            jax.ShapeDtypeStruct((len(RIGHT), rows, block), BF16),
            jax.ShapeDtypeStruct((len(LEFT), rows, block), BF16),
            jax.ShapeDtypeStruct((rows // 2, block), BF16),
            jax.ShapeDtypeStruct((rows // 2, block), BF16),
            jax.ShapeDtypeStruct((len(KEEP), rows, block), F32),
        ),
        in_specs=[pl.BlockSpec(memory_space=pltpu.SMEM)] + vmem_specs(2),
        out_specs=tuple(vmem_specs(5)),
        cost_estimate=pl.CostEstimate(flops=mine.size, bytes_accessed=8 * mine.size, transcendentals=0),
        compiler_params=GRANT,
        name="pair_sum",
    )(z, mine, other)


def relay_kernel(
    keep_ref, right_ref, left_ref, half_right_ref, half_left_ref, here_ref, far_right_ref, far_left_ref
):
    rows = here_ref.shape[0]
    half = rows // 2
    here_ref[...] = keep_ref[0] + right_ref[0].astype(F32) + left_ref[0].astype(F32)
    for first, last in ((0, half), (half, rows)):
        right = keep_ref[1, first:last] + right_ref[1, first:last].astype(F32)
        left = keep_ref[2, first:last] + left_ref[1, first:last].astype(F32)
        if first == 0:
            right += half_right_ref[...].astype(F32)
        else:
            left += half_left_ref[...].astype(F32)
        far_right_ref[first:last] = right.astype(BF16)
        far_left_ref[first:last] = left.astype(BF16)


def relay(keep, right, left, half_right, half_left):
    _, rows, block = keep.shape
    return pl.pallas_call(
        relay_kernel,
        out_shape=(
            jax.ShapeDtypeStruct((rows, block), F32),
            jax.ShapeDtypeStruct((rows, block), BF16),
            jax.ShapeDtypeStruct((rows, block), BF16),
        ),
        in_specs=vmem_specs(5),
        out_specs=tuple(vmem_specs(3)),
        cost_estimate=pl.CostEstimate(flops=5 * rows * block, bytes_accessed=4 * keep.size, transcendentals=0),
        compiler_params=GRANT,
        name="relay",
    )(keep, right, left, half_right, half_left)


def wanted_row(slots_ref, width):
    tags = slots_ref[:, width:].astype(F32)
    return tags.T[0:1, :]


def shrink_kernel(owned, slots_ref, down_ref, out_ref):
    slot_total = slots_ref.shape[0]
    width = down_ref.shape[1]
    rank = down_ref.shape[0] // owned
    terms = lax.dot_general(
        down_ref[...], slots_ref[:, :width], (((1,), (1,)), ((), ())), preferred_element_type=F32
    )
    wanted = wanted_row(slots_ref, width)
    total = jnp.zeros((rank, slot_total), F32)
    for adapter in range(owned):
        total += jnp.where(wanted == adapter + 1, terms[adapter * rank : (adapter + 1) * rank], 0.0)
    out_ref[...] = total


def shrink_terms(slots, down, owned):
    slot_total = slots.shape[0]
    rank = down.shape[0] // owned
    return pl.pallas_call(
        functools.partial(shrink_kernel, owned),
        out_shape=jax.ShapeDtypeStruct((rank, slot_total), F32),
        in_specs=vmem_specs(2),
        out_specs=pl.BlockSpec(memory_space=pltpu.VMEM),
        cost_estimate=pl.CostEstimate(
            flops=2 * slot_total * down.size, bytes_accessed=2 * down.size, transcendentals=0
        ),
        compiler_params=GRANT,
        name="shrink",
    )(slots, down)


def expand_kernel(owned, three_ref, right_ref, left_ref, slots_ref, up_ref, out_ref):
    total = three_ref[...] + right_ref[...] + left_ref[...]
    shrink = total.astype(BF16).astype(F32)
    wanted = wanted_row(slots_ref, slots_ref.shape[1] - LANES)
    spread = jnp.concatenate(
        [jnp.where(wanted == adapter + 1, shrink, 0.0).astype(BF16) for adapter in range(owned)], axis=0
    )
    out_ref[...] = lax.dot_general(
        spread, up_ref[...], (((0,), (0,)), ((), ())), preferred_element_type=F32
    ).astype(BF16)


def expand_rows(three, right, left, slots, up, owned):
    slot_total = slots.shape[0]
    return pl.pallas_call(
        functools.partial(expand_kernel, owned),
        out_shape=jax.ShapeDtypeStruct((slot_total, up.shape[1]), BF16),
        in_specs=vmem_specs(5),
        out_specs=pl.BlockSpec(memory_space=pltpu.VMEM),
        cost_estimate=pl.CostEstimate(
            flops=10**11, bytes_accessed=10**9, transcendentals=0
        ),
        compiler_params=GRANT,
        name="expand",
    )(three, right, left, slots, up)


def finish_kernel(
    owned, capacity, index_ref, here_ref, right_ref, left_ref, returned_ref, out_ref
):
    rows = here_ref.shape[0]
    slot_count = returned_ref.shape[0]
    slot = slots_of(index_ref[...], owned, capacity)
    placing = lax.broadcasted_iota(jnp.int32, (slot_count, rows), 0) == slot
    branch = lax.dot_general(
        jnp.where(placing, 1.0, 0.0).astype(BF16),
        returned_ref[...],
        (((0,), (0,)), ((), ())),
        preferred_element_type=F32,
    )
    base = here_ref[...] + right_ref[...].astype(F32) + left_ref[...].astype(F32)
    out_ref[...] = (base + branch).astype(BF16)


def finish(index_row, sums, returned, owned, capacity):
    return pl.pallas_call(
        functools.partial(finish_kernel, owned, capacity),
        out_shape=jax.ShapeDtypeStruct(sums[0].shape, BF16),
        in_specs=vmem_specs(5),
        out_specs=pl.BlockSpec(memory_space=pltpu.VMEM),
        cost_estimate=pl.CostEstimate(
            flops=2 * returned.size * sums[0].shape[0], bytes_accessed=8 * sums[0].size, transcendentals=0
        ),
        compiler_params=GRANT,
        name="finish",
    )(index_row, *sums, returned)


def body(attention_output, residual, output_weight, down_factors, up_factors, adapter_index):
    rows, width = attention_output.shape
    owned, _, rank = down_factors.shape
    columns = up_factors.shape[2]
    groups = lax.axis_size("dp")
    shards = lax.axis_size("tensor")
    chips = shards // 2
    capacity = 2 * rows // groups
    slot_count = groups * capacity
    place = lax.axis_index("tensor")
    z, place = (place >> 1).reshape(1), place.reshape(1)
    siblings = [(i, i ^ 1) for i in range(shards)]

    def along_z(array, step):
        return lax.ppermute(array, "tensor", [(i, (i + 2 * step) % shards) for i in range(shards)])

    index_row = adapter_index.reshape(1, rows)
    outgoing = dispatch(index_row, attention_output, owned, capacity, slot_count)
    outgoing, x = lax.optimization_barrier((outgoing, attention_output))
    outgoing = outgoing.reshape(groups, capacity, width + LANES)
    slots = lax.all_to_all(outgoing, "dp", split_axis=0, concat_axis=0, tiled=True)

    theirs, mine = product(place, x, residual, output_weight, chips)
    slots, theirs, mine = lax.optimization_barrier((slots, theirs, mine))

    slots = slots.reshape(slot_count, width + LANES)
    down = down_factors.transpose(0, 2, 1).reshape(owned * rank, width)
    shrink = shrink_terms(slots, down, owned)
    both = shrink + lax.ppermute(shrink, "tensor", siblings)
    both, theirs = lax.optimization_barrier((both, theirs))
    other = lax.ppermute(theirs, "tensor", siblings)
    *moving, keep = pair_sum(z, mine, other)
    before, after = along_z(both, 1), along_z(both, -1)
    before, after, *moving = lax.optimization_barrier((before, after, *moving))
    two = both + before
    three = two + after
    three_left, two_right = along_z(three, 3), along_z(two, -3)
    halves = along_z(moving[2], 2), along_z(moving[3], -2)
    three_left, *halves = lax.optimization_barrier((three_left, *halves))
    arrived = along_z(moving[0], 1), along_z(moving[1], -1), *halves
    here, far_right, far_left = relay(keep, *arrived)
    sums = (here, along_z(far_right, 2), along_z(far_left, -2))
    up = up_factors.reshape(owned * rank, columns)
    expand = expand_rows(three, three_left, two_right, slots, up, owned)
    expand = expand.reshape(groups, capacity, columns)
    returned = lax.all_to_all(expand, "dp", split_axis=0, concat_axis=0, tiled=True)
    returned = returned.reshape(slot_count, columns)
    return finish(index_row, sums, returned, owned, capacity)


def solution(mesh):
    return jax.shard_map(
        body,
        mesh=mesh,
        in_specs=(
            P("dp", "tensor"),
            P("dp", "tensor"),
            P("tensor", None),
            P("dp", "tensor", None),
            P("dp", None, "tensor"),
            P("dp"),
        ),
        out_specs=P("dp", "tensor"),
        check_vma=False,
    )
```

```python
import functools

import jax
import jax.numpy as jnp
from jax import lax
from jax.experimental import pallas as pl
from jax.experimental.pallas import tpu as pltpu
from jax.sharding import PartitionSpec as P

BF16 = jnp.bfloat16
F32 = jnp.float32
LANES = 128
RIGHT = (1, 3)
LEFT = (-1, -3)
KEEP = (0, 2, -2)
PIECES = (0, 4, 6, 8)
GRANT = pltpu.CompilerParams(vmem_limit_bytes=16 * 2**20)
WHOLE = pltpu.CompilerParams(vmem_limit_bytes=60 * 2**20)


def vmem_specs(count):
    return [pl.BlockSpec(memory_space=pltpu.VMEM)] * count


def slots_of(index_row, owned, capacity):
    rows = index_row.shape[1]
    owner = index_row // owned
    owner_across = jnp.broadcast_to(owner, (rows, rows))
    owner_down = owner_across.T
    earlier = lax.broadcasted_iota(jnp.int32, (rows, rows), 0) < lax.broadcasted_iota(
        jnp.int32, (rows, rows), 1
    )
    same = jnp.where((owner_down == owner_across) & earlier, 1, 0)
    rank = jnp.sum(same, axis=0, keepdims=True)
    return owner * capacity + rank


def dispatch_kernel(owned, capacity, index_ref, x_ref, out_ref):
    index_row = index_ref[...]
    rows, width = x_ref.shape
    slot_count = out_ref.shape[0]
    slot = slots_of(index_row, owned, capacity)
    placing = lax.broadcasted_iota(jnp.int32, (slot_count, rows), 0) == slot
    out_ref[:, :width] = jnp.dot(
        jnp.where(placing, 1.0, 0.0).astype(BF16), x_ref[...], preferred_element_type=F32
    ).astype(BF16)
    number = (index_row % owned + 1).astype(F32)
    asked = jnp.sum(jnp.where(placing, number, 0.0), axis=1, keepdims=True)
    out_ref[:, width:] = jnp.broadcast_to(asked, (slot_count, LANES)).astype(BF16)


def dispatch(index_row, x, owned, capacity, slot_count):
    rows, width = x.shape
    return pl.pallas_call(
        functools.partial(dispatch_kernel, owned, capacity),
        out_shape=jax.ShapeDtypeStruct((slot_count, width + LANES), BF16),
        in_specs=vmem_specs(2),
        out_specs=pl.BlockSpec(memory_space=pltpu.VMEM),
        cost_estimate=pl.CostEstimate(
            flops=2 * slot_count * rows * width, bytes_accessed=2 * slot_count * width, transcendentals=0
        ),
        compiler_params=WHOLE,
        name="dispatch",
    )(index_row, x)


def product_kernel(
    place_ref,
    x_hbm,
    residual_hbm,
    w_hbm,
    theirs_hbm,
    mine_hbm,
    x_ref,
    residual_ref,
    w_ref,
    theirs_ref,
    mine_ref,
    x_sem,
    residual_sem,
    w_sems,
    out_sems,
):
    here, first = place_ref[0] >> 1, (place_ref[0] & 1) == 0
    chips, _, block = mine_ref.shape
    loads = [pltpu.make_async_copy(x_hbm, x_ref, x_sem)]
    part = w_ref.shape[1] // chips
    for piece, (start, stop) in enumerate(zip(PIECES, PIECES[1:])):
        columns = slice(start * part, stop * part)
        loads.append(
            pltpu.make_async_copy(w_hbm.at[:, columns], w_ref.at[:, columns], w_sems.at[piece])
        )
    for load in loads:
        load.start()
    residual_load = pltpu.make_async_copy(residual_hbm, residual_ref, residual_sem)
    residual_load.start()
    loads[0].wait()
    stores = []
    for z in range(chips):
        if z in PIECES:
            loads[1 + PIECES.index(z)].wait()
        if z == 0:
            residual_load.wait()
        both = jnp.dot(
            x_ref[...], w_ref[:, 2 * z * block : 2 * (z + 1) * block], preferred_element_type=F32
        )
        low, high = both[:, :block], both[:, block:]
        theirs_ref[z] = jnp.where(first, high, low).astype(BF16)
        mine_ref[z] = jnp.where(first, low, high) + jnp.where(here == z, residual_ref[...].astype(F32), 0.0)
        for place, (ref, hbm) in enumerate(((theirs_ref, theirs_hbm), (mine_ref, mine_hbm))):
            stores.append(pltpu.make_async_copy(ref.at[z], hbm.at[z], out_sems.at[place, z]))
            stores[-1].start()
    for store in stores:
        store.wait()


def product(place, x, residual, w, chips):
    rows, depth = x.shape
    block = w.shape[1] // (2 * chips)
    anywhere = pl.BlockSpec(memory_space=pl.ANY)
    return pl.pallas_call(
        product_kernel,
        out_shape=(
            jax.ShapeDtypeStruct((chips, rows, block), BF16),
            jax.ShapeDtypeStruct((chips, rows, block), F32),
        ),
        in_specs=[pl.BlockSpec(memory_space=pltpu.SMEM), anywhere, anywhere, anywhere],
        out_specs=(anywhere, anywhere),
        scratch_shapes=[
            pltpu.VMEM(x.shape, BF16),
            pltpu.VMEM(residual.shape, BF16),
            pltpu.VMEM(w.shape, BF16),
            pltpu.VMEM((chips, rows, block), BF16),
            pltpu.VMEM((chips, rows, block), F32),
            pltpu.SemaphoreType.DMA,
            pltpu.SemaphoreType.DMA,
            pltpu.SemaphoreType.DMA((len(PIECES) - 1,)),
            pltpu.SemaphoreType.DMA((2, chips)),
        ],
        cost_estimate=pl.CostEstimate(
            flops=2 * rows * w.size, bytes_accessed=2 * w.size, transcendentals=0
        ),
        compiler_params=WHOLE,
        name="product",
    )(place, x, residual, w)


def pair_kernel(
    chips, z_ref, mine_ref, other_ref, right_ref, left_ref, half_right_ref, half_left_ref, keep_ref
):
    z = z_ref[0]
    rows = keep_ref.shape[1]
    half = rows // 2

    def total(step, first, last):
        at = lax.rem(z + (step + chips), chips)
        return mine_ref[at, first:last] + other_ref[at, first:last].astype(F32)

    for ref, steps in ((right_ref, RIGHT), (left_ref, LEFT)):
        for place, step in enumerate(steps):
            ref[place] = total(step, 0, rows).astype(BF16)
    half_right_ref[...] = total(chips // 2, 0, half).astype(BF16)
    half_left_ref[...] = total(chips // 2, half, rows).astype(BF16)
    for place, step in enumerate(KEEP):
        keep_ref[place] = total(step, 0, rows)


def pair_sum(z, mine, other):
    chips, rows, block = mine.shape
    return pl.pallas_call(
        functools.partial(pair_kernel, chips),
        out_shape=(
            jax.ShapeDtypeStruct((len(RIGHT), rows, block), BF16),
            jax.ShapeDtypeStruct((len(LEFT), rows, block), BF16),
            jax.ShapeDtypeStruct((rows // 2, block), BF16),
            jax.ShapeDtypeStruct((rows // 2, block), BF16),
            jax.ShapeDtypeStruct((len(KEEP), rows, block), F32),
        ),
        in_specs=[pl.BlockSpec(memory_space=pltpu.SMEM)] + vmem_specs(2),
        out_specs=tuple(vmem_specs(5)),
        cost_estimate=pl.CostEstimate(flops=mine.size, bytes_accessed=8 * mine.size, transcendentals=0),
        compiler_params=GRANT,
        name="pair_sum",
    )(z, mine, other)


def relay_kernel(
    keep_ref, right_ref, left_ref, half_right_ref, half_left_ref, here_ref, far_right_ref, far_left_ref
):
    rows = here_ref.shape[0]
    half = rows // 2
    here_ref[...] = keep_ref[0] + right_ref[0].astype(F32) + left_ref[0].astype(F32)
    for first, last in ((0, half), (half, rows)):
        right = keep_ref[1, first:last] + right_ref[1, first:last].astype(F32)
        left = keep_ref[2, first:last] + left_ref[1, first:last].astype(F32)
        if first == 0:
            right += half_right_ref[...].astype(F32)
        else:
            left += half_left_ref[...].astype(F32)
        far_right_ref[first:last] = right.astype(BF16)
        far_left_ref[first:last] = left.astype(BF16)


def relay(keep, right, left, half_right, half_left):
    _, rows, block = keep.shape
    return pl.pallas_call(
        relay_kernel,
        out_shape=(
            jax.ShapeDtypeStruct((rows, block), F32),
            jax.ShapeDtypeStruct((rows, block), BF16),
            jax.ShapeDtypeStruct((rows, block), BF16),
        ),
        in_specs=vmem_specs(5),
        out_specs=tuple(vmem_specs(3)),
        cost_estimate=pl.CostEstimate(flops=5 * rows * block, bytes_accessed=4 * keep.size, transcendentals=0),
        compiler_params=GRANT,
        name="relay",
    )(keep, right, left, half_right, half_left)


def wanted_row(slots_ref, width):
    tags = slots_ref[:, width:].astype(F32)
    return tags.T[0:1, :]


def shrink_kernel(owned, slots_ref, down_ref, out_ref):
    slot_total = slots_ref.shape[0]
    width = down_ref.shape[1]
    rank = down_ref.shape[0] // owned
    terms = lax.dot_general(
        down_ref[...], slots_ref[:, :width], (((1,), (1,)), ((), ())), preferred_element_type=F32
    )
    wanted = wanted_row(slots_ref, width)
    total = jnp.zeros((rank, slot_total), F32)
    for adapter in range(owned):
        total += jnp.where(wanted == adapter + 1, terms[adapter * rank : (adapter + 1) * rank], 0.0)
    out_ref[...] = total


def shrink_terms(slots, down, owned):
    slot_total = slots.shape[0]
    rank = down.shape[0] // owned
    return pl.pallas_call(
        functools.partial(shrink_kernel, owned),
        out_shape=jax.ShapeDtypeStruct((rank, slot_total), F32),
        in_specs=vmem_specs(2),
        out_specs=pl.BlockSpec(memory_space=pltpu.VMEM),
        cost_estimate=pl.CostEstimate(
            flops=2 * slot_total * down.size, bytes_accessed=2 * down.size, transcendentals=0
        ),
        compiler_params=GRANT,
        name="shrink",
    )(slots, down)


def expand_kernel(owned, three_ref, right_ref, left_ref, slots_ref, up_ref, out_ref):
    total = three_ref[...] + right_ref[...] + left_ref[...]
    shrink = total.astype(BF16).astype(F32)
    wanted = wanted_row(slots_ref, slots_ref.shape[1] - LANES)
    spread = jnp.concatenate(
        [jnp.where(wanted == adapter + 1, shrink, 0.0).astype(BF16) for adapter in range(owned)], axis=0
    )
    out_ref[...] = lax.dot_general(
        spread, up_ref[...], (((0,), (0,)), ((), ())), preferred_element_type=F32
    ).astype(BF16)


def expand_rows(three, right, left, slots, up, owned):
    slot_total = slots.shape[0]
    return pl.pallas_call(
        functools.partial(expand_kernel, owned),
        out_shape=jax.ShapeDtypeStruct((slot_total, up.shape[1]), BF16),
        in_specs=vmem_specs(5),
        out_specs=pl.BlockSpec(memory_space=pltpu.VMEM),
        cost_estimate=pl.CostEstimate(
            flops=10**11, bytes_accessed=10**9, transcendentals=0
        ),
        compiler_params=GRANT,
        name="expand",
    )(three, right, left, slots, up)


def finish_kernel(
    owned, capacity, index_ref, here_ref, right_ref, left_ref, returned_ref, out_ref
):
    rows = here_ref.shape[0]
    slot_count = returned_ref.shape[0]
    slot = slots_of(index_ref[...], owned, capacity)
    placing = lax.broadcasted_iota(jnp.int32, (slot_count, rows), 0) == slot
    branch = lax.dot_general(
        jnp.where(placing, 1.0, 0.0).astype(BF16),
        returned_ref[...],
        (((0,), (0,)), ((), ())),
        preferred_element_type=F32,
    )
    base = here_ref[...] + right_ref[...].astype(F32) + left_ref[...].astype(F32)
    out_ref[...] = (base + branch).astype(BF16)


def finish(index_row, sums, returned, owned, capacity):
    return pl.pallas_call(
        functools.partial(finish_kernel, owned, capacity),
        out_shape=jax.ShapeDtypeStruct(sums[0].shape, BF16),
        in_specs=vmem_specs(5),
        out_specs=pl.BlockSpec(memory_space=pltpu.VMEM),
        cost_estimate=pl.CostEstimate(
            flops=2 * returned.size * sums[0].shape[0], bytes_accessed=8 * sums[0].size, transcendentals=0
        ),
        compiler_params=GRANT,
        name="finish",
    )(index_row, *sums, returned)


def body(attention_output, residual, output_weight, down_factors, up_factors, adapter_index):
    rows, width = attention_output.shape
    owned, _, rank = down_factors.shape
    columns = up_factors.shape[2]
    groups = lax.axis_size("dp")
    shards = lax.axis_size("tensor")
    chips = shards // 2
    capacity = 2 * rows // groups
    slot_count = groups * capacity
    place = lax.axis_index("tensor")
    z, place = (place >> 1).reshape(1), place.reshape(1)
    siblings = [(i, i ^ 1) for i in range(shards)]

    def along_z(array, step):
        return lax.ppermute(array, "tensor", [(i, (i + 2 * step) % shards) for i in range(shards)])

    index_row = adapter_index.reshape(1, rows)
    outgoing = dispatch(index_row, attention_output, owned, capacity, slot_count)
    outgoing, x = lax.optimization_barrier((outgoing, attention_output))
    outgoing = outgoing.reshape(groups, capacity, width + LANES)
    slots = lax.all_to_all(outgoing, "dp", split_axis=0, concat_axis=0, tiled=True)

    theirs, mine = product(place, x, residual, output_weight, chips)
    slots, theirs, mine = lax.optimization_barrier((slots, theirs, mine))

    slots = slots.reshape(slot_count, width + LANES)
    down = down_factors.transpose(0, 2, 1).reshape(owned * rank, width)
    shrink = shrink_terms(slots, down, owned)
    both = shrink + lax.ppermute(shrink, "tensor", siblings)
    both, theirs = lax.optimization_barrier((both, theirs))
    other = lax.ppermute(theirs, "tensor", siblings)
    *moving, keep = pair_sum(z, mine, other)
    before, after = along_z(both, 1), along_z(both, -1)
    before, after, *moving = lax.optimization_barrier((before, after, *moving))
    two = both + before
    three = two + after
    three_left, two_right = along_z(three, 3), along_z(two, -3)
    halves = along_z(moving[2], 2), along_z(moving[3], -2)
    three_left, *halves = lax.optimization_barrier((three_left, *halves))
    arrived = along_z(moving[0], 1), along_z(moving[1], -1), *halves
    here, far_right, far_left = relay(keep, *arrived)
    sums = (here, along_z(far_right, 2), along_z(far_left, -2))
    up = up_factors.reshape(owned * rank, columns)
    expand = expand_rows(three, three_left, two_right, slots, up, owned)
    expand = expand.reshape(groups, capacity, columns)
    returned = lax.all_to_all(expand, "dp", split_axis=0, concat_axis=0, tiled=True)
    returned = returned.reshape(slot_count, columns)
    return finish(index_row, sums, returned, owned, capacity)


def solution(mesh):
    return jax.shard_map(
        body,
        mesh=mesh,
        in_specs=(
            P("dp", "tensor"),
            P("dp", "tensor"),
            P("tensor", None),
            P("dp", "tensor", None),
            P("dp", None, "tensor"),
            P("dp"),
        ),
        out_specs=P("dp", "tensor"),
        check_vma=False,
    )
```
